32 devices in a mesh: pb: 2 (over core), ka: 16 (over z, y, x).
Axes of the slice: x: 2, y: 2, z: 4, core: 2. Of those that a mesh axis runs over, the one named last changes fastest.
Arguments:
- vertex_ladder: float32 [2, 8, 1024, 1024], P(None, 'pb', 'ka'), may hold values from -6 to 6
- vertex_cross_a: float32 [2, 8, 1024, 1024], P(None, 'pb', 'ka'), may hold values from -6 to 6
- vertex_cross_b: float32 [2, 8, 1024, 1024], P(None, 'pb', 'ka'), may hold values from -6 to 6
- bubble: float32 [2, 8, 1024], P(None, 'pb'), may hold values from -0.072 to 0.072
- row_maps: int32 [2, 8, 1024], replicated, may hold values from 0 to 8191, as said below
- col_maps: int32 [2, 1024], replicated, may hold values from 0 to 1023, each once within a row
Outputs:
- ladder_out: float32 [2, 8, 1024, 1024], P(None, 'pb', 'ka')
- crossed_a: float32 [2, 8, 1024, 1024], P(None, 'pb', 'ka')
- crossed_b: float32 [2, 8, 1024, 1024], P(None, 'pb', 'ka')
The draws below stay inside these ranges and needn't reach their ends.
Inputs may be any that keep to these rules, and one draw needn't show every extreme that they name: `row_maps`: each of the two maps is a permutation of all 8192 rows. A device holds the rows of its bosonic indices (index of pb) and its first fermionic indices (index of ka); the 256 rows of one device take exactly 8 of their source rows from each device.
All inputs are finite; a program needn't handle non-finite values.
Results may differ from the reference program's by a relative error of at most 0.007.
Values may be sent and summed in bfloat16 or wider, within the bound.
No kernel may reach another device: no remote copies, remote signals or barrier semaphores. Data moves between devices by JAX's collectives and lax.ppermute only.
A program may use at most 64 MiB of HBM per device.

```python
import jax
import jax.numpy as jnp
from jax import lax

K = 1024
Q_DEV = 4
LADDER = 6
Q = 8
ROWS = 64
DEVS = 32


def one_table(key):
    key_target, key_offset, key_source = jax.random.split(key, 3)
    count = Q_DEV * K // (K // ROWS)
    per_peer = count // DEVS
    ka_count = K // ROWS
    target_perm = jax.vmap(lambda sub: jax.random.permutation(sub, count))(jax.random.split(key_target, DEVS))
    offsets = jax.random.randint(key_offset, (DEVS,), 0, DEVS)
    source_perm = jax.vmap(lambda sub: jax.random.permutation(sub, count))(jax.random.split(key_source, DEVS))
    device_ids = jnp.arange(DEVS, dtype=jnp.int32)[:, None]
    source_dev = (target_perm % DEVS + offsets[:, None]) % DEVS
    source_slot = device_ids * per_peer + target_perm // DEVS
    source_local = source_perm[source_dev, source_slot]
    local_ids = jnp.arange(count, dtype=jnp.int32)[None, :]

    def global_row(device, local):
        bos = device // ka_count * Q_DEV + local // ROWS
        fer = device % ka_count * ROWS + local % ROWS
        return (bos * K + fer).astype(jnp.int32)
    target_rows = global_row(device_ids + 0 * local_ids, local_ids + 0 * device_ids).reshape(-1)
    source_rows = global_row(source_dev, source_local).reshape(-1)
    table = jnp.zeros((Q * K,), jnp.int32).at[target_rows].set(source_rows)
    return table.reshape(Q, K)


def draw_row_maps(key, part):
    return jnp.stack([one_table(jax.random.fold_in(key, 11)), one_table(jax.random.fold_in(key, 23))])


def level_of(key, extent, cuts, smallest, largest):
    def one(dim, blocks):
        steps = jax.random.uniform(jax.random.fold_in(jax.random.fold_in(key, 6), dim), (blocks,), jnp.float32, smallest / len(cuts), largest / len(cuts))
        return jnp.repeat(jnp.exp(steps), extent[dim] // blocks).reshape((-1,) + (1,) * (len(extent) - dim - 1))

    gain = one(*cuts[0])
    for cut in cuts[1:]:
        gain = gain * one(*cut)
    return gain


def noise(own_key, extent, width, most, pieces=(), kind=jnp.bfloat16):
    drawn = width * jax.random.normal(own_key, extent, jnp.float32)
    if pieces:
        drawn = drawn * level_of(own_key, extent, pieces, -0.22, 0.18)
    return jnp.clip(drawn, -most, most).astype(kind)


def setup_inputs(seed: int = 0) -> dict:
    splits = jax.random.split(jax.random.key(seed), 7)
    vertex_ladder = noise(splits[0], (2, Q, K, K), 1.0, 6.0, ((1, 2), (2, 16)), jnp.float32)
    vertex_cross_a = noise(splits[1], (2, Q, K, K), 1.0, 6.0, ((1, 2), (2, 16)), jnp.float32)
    vertex_cross_b = noise(splits[2], (2, Q, K, K), 1.0, 6.0, ((1, 2), (2, 16)), jnp.float32)
    bubble = noise(splits[3], (2, Q, K), 0.012, 0.072, ((1, 2),), jnp.float32)
    row_maps = draw_row_maps(jax.random.fold_in(splits[6], 71), 0)
    col_maps = jax.vmap(lambda own: jax.random.permutation(own, K))(jax.random.split(splits[5], 2)).reshape((2, K)).astype(jnp.int32)
    return {"vertex_ladder": vertex_ladder, "vertex_cross_a": vertex_cross_a, "vertex_cross_b": vertex_cross_b, "bubble": bubble, "row_maps": row_maps, "col_maps": col_maps}


def ladder_one(operands):
    vertex_q, bubble_q = operands
    lowered = vertex_q.astype(jnp.bfloat16)
    right_op = jnp.concatenate([lowered[0], lowered[1]], 1)
    row_count = vertex_q.shape[1]
    current = vertex_q
    for _ in range(LADDER):
        scaled_re = current[0] * bubble_q[0][None, :] - current[1] * bubble_q[1][None, :]
        scaled_im = current[0] * bubble_q[1][None, :] + current[1] * bubble_q[0][None, :]
        left_op = jnp.concatenate([scaled_re, scaled_im], 0).astype(jnp.bfloat16)
        product = jnp.dot(left_op, right_op, preferred_element_type=jnp.float32)
        real_part = product[:row_count, :K] - product[row_count:, K:]
        imag_part = product[:row_count, K:] + product[row_count:, :K]
        current = vertex_q + jnp.stack([real_part, imag_part])
    return current


def reference(vertex_ladder, vertex_cross_a, vertex_cross_b, bubble, row_maps, col_maps):
    full = lax.map(ladder_one, (jnp.moveaxis(vertex_ladder, 1, 0), jnp.moveaxis(bubble, 1, 0)))
    ladder_out = jnp.moveaxis(full, 0, 1)
    reducible = (ladder_out - vertex_ladder).reshape(2, Q * K, K)

    def cross(channel, base):
        picked = jnp.take(reducible, row_maps[channel].reshape(-1).astype(jnp.int32), axis=1)
        picked = jnp.take(picked, col_maps[channel].astype(jnp.int32), axis=2)
        return base + picked.reshape(2, Q, K, K)

    return ladder_out, cross(0, vertex_cross_a), cross(1, vertex_cross_b)
```

```python
import functools

import jax
import jax.numpy as jnp
from jax import lax
from jax.experimental import pallas as pl
from jax.experimental.pallas import tpu as pltpu
from jax.sharding import PartitionSpec as P

LADDER = 6
TILE = 256


def ladder_kernel(groups, plane, place_ref, chi_ref, *refs):
    pieces = refs[: groups * plane]
    outs = refs[groups * plane : groups * plane + groups]
    right, left, base, sems = refs[groups * plane + groups :]
    rows = pieces[0].shape[1]
    depth = pieces[0].shape[2]
    count = groups * rows
    group, member = place_ref[0], place_ref[1]
    copies = []
    for d in range(groups):
        for e in range(plane):
            source = lax.bitwise_xor(group, d) * plane + lax.bitwise_xor(member, e)
            start = pl.multiple_of(source * rows, rows)
            for part in range(2):
                copy = pltpu.make_async_copy(
                    pieces[d * plane + e].at[part],
                    right.at[pl.ds(part * depth + start, rows), :],
                    sems.at[(d * plane + e) * 2 + part],
                )
                copy.start()
                copies.append(copy)
    for copy in copies:
        copy.wait()
    for d in range(groups):
        source = lax.bitwise_xor(group, d) * plane + member
        start = pl.multiple_of(source * rows, rows)
        for part in range(2):
            base[pl.ds(part * count + d * rows, rows), :] = right[
                pl.ds(part * depth + start, rows), :
            ]

    def scaled(slot, columns, real, imag):
        chi_re, chi_im = chi_ref[0:1, columns], chi_ref[1:2, columns]
        scaled_re = real * chi_re - imag * chi_im
        scaled_im = real * chi_im + imag * chi_re
        low_re = scaled_re.astype(jnp.bfloat16)
        low_im = scaled_im.astype(jnp.bfloat16)
        shifted = slice(columns.start + depth, columns.stop + depth)
        left[slot, :count, columns] = low_re
        left[slot, count:, columns] = low_im
        left[slot, count:, shifted] = low_re
        left[slot, :count, shifted] = -low_im

    tiles = [slice(j * TILE, (j + 1) * TILE) for j in range(depth // TILE)]
    for columns in tiles:
        whole = base[:, columns].astype(jnp.float32)
        scaled(0, columns, whole[:count], whole[count:])
    for step in range(LADDER):
        for columns in tiles:
            product = jnp.dot(
                left[step % 2], right[:, columns], preferred_element_type=jnp.float32
            )
            if step < LADDER - 1:
                whole = product + base[:, columns].astype(jnp.float32)
                scaled((step + 1) % 2, columns, whole[:count], whole[count:])
            else:
                low = product.astype(jnp.bfloat16)
                for d in range(groups):
                    for part in range(2):
                        start = part * count + d * rows
                        outs[d][part, :, columns] = low[start : start + rows]


def ladder(place, chi, pieces, groups, plane):
    _, rows, depth = pieces[0].shape
    count = groups * rows
    return pl.pallas_call(
        functools.partial(ladder_kernel, groups, plane),
        out_shape=[jax.ShapeDtypeStruct((2, rows, depth), jnp.bfloat16)] * groups,
        in_specs=[
            pl.BlockSpec(memory_space=pltpu.SMEM),
            pl.BlockSpec(memory_space=pltpu.VMEM),
        ]
        + [pl.BlockSpec(memory_space=pl.ANY)] * (groups * plane),
        out_specs=[pl.BlockSpec(memory_space=pltpu.VMEM)] * groups,
        scratch_shapes=[
            pltpu.VMEM((2 * depth, depth), jnp.bfloat16),
            pltpu.VMEM((2, 2 * count, 2 * depth), jnp.bfloat16),
            pltpu.VMEM((2 * count, depth), jnp.bfloat16),
            pltpu.SemaphoreType.DMA((groups * plane * 2,)),
        ],
        cost_estimate=pl.CostEstimate(
            flops=LADDER * 8 * count * depth * depth,
            bytes_accessed=4 * depth * depth + 8 * count * depth,
            transcendentals=0,
        ),
        name="ladder",
    )(place, chi, *pieces)


def select_kernel(chosen_ref, *refs):
    groups = len(refs) - 1
    out = refs[-1]
    depth = refs[0].shape[2]
    for part in range(2):
        rows = jnp.concatenate([refs[d][part] for d in range(groups)], 0)
        out[:, part * depth : (part + 1) * depth] = jnp.dot(
            chosen_ref[...], rows, preferred_element_type=jnp.float32
        ).astype(jnp.bfloat16)


def select_rows(chosen, returned):
    _, _, depth = returned[0].shape
    return pl.pallas_call(
        select_kernel,
        out_shape=jax.ShapeDtypeStruct((chosen.shape[0], 2 * depth), jnp.bfloat16),
        cost_estimate=pl.CostEstimate(
            flops=4 * chosen.shape[0] * chosen.shape[1] * depth,
            bytes_accessed=8 * chosen.shape[0] * depth,
            transcendentals=0,
        ),
        name="select_rows",
    )(chosen, *returned)


def place_kernel(rows_ref, columns_ref, received_ref, base_ref, out_ref):
    picked = jnp.dot(
        rows_ref[...], received_ref[...], preferred_element_type=jnp.float32
    ).astype(jnp.bfloat16)
    out_ref[0] = base_ref[0] + jnp.dot(
        picked, columns_ref[...], preferred_element_type=jnp.float32
    )


def place_rows(row_pick, column_pick, received, base):
    count, slots = row_pick.shape
    depth = column_pick.shape[0]
    return pl.pallas_call(
        place_kernel,
        out_shape=jax.ShapeDtypeStruct((2, count, depth), jnp.float32),
        grid=(2,),
        in_specs=[
            pl.BlockSpec((count, slots), lambda part: (0, 0)),
            pl.BlockSpec((depth, depth), lambda part: (0, 0)),
            pl.BlockSpec((slots, depth), lambda part: (0, part)),
            pl.BlockSpec((1, count, depth), lambda part: (part, 0, 0)),
        ],
        out_specs=pl.BlockSpec((1, count, depth), lambda part: (part, 0, 0)),
        cost_estimate=pl.CostEstimate(
            flops=4 * count * depth * (slots + depth),
            bytes_accessed=16 * count * depth + 2 * depth * depth,
            transcendentals=0,
        ),
        name="place_rows",
    )(row_pick, column_pick, received, base)


def per_device(vertex_ladder, vertex_cross_a, vertex_cross_b, bubble, row_maps, col_maps):
    _, q_local, row_count, col_count = vertex_ladder.shape
    pb_count = lax.axis_size("pb")
    ka_count = lax.axis_size("ka")
    plane = ka_count // q_local
    my_pb = lax.axis_index("pb")
    my_ka = lax.axis_index("ka")
    group = my_ka // plane
    member = my_ka % plane
    local_count = q_local * row_count
    dev_count = pb_count * ka_count
    per_peer = local_count // dev_count
    my_device = my_pb * ka_count + my_ka

    def swap(value, mask):
        return lax.ppermute(value, "ka", [(i, i ^ mask) for i in range(ka_count)])

    gamma_low = vertex_ladder.astype(jnp.bfloat16)

    def piece_of(index):
        return lax.dynamic_index_in_dim(gamma_low, index, 1, keepdims=False)

    held = {}
    for d in [*range(q_local - 1, 0, -1)]:
        held[d, 0] = swap(piece_of(group ^ d), d * plane)
    held[0, 0] = piece_of(group)
    bits = [1 << b for b in range(plane.bit_length() - 1)]
    for d in range(q_local):
        order = bits if d % 2 == 0 else bits[::-1]
        have = [0]
        for bit in order:
            for e in have:
                held[d, e ^ bit] = swap(held[d, e], bit)
            have = have + [e ^ bit for e in have]
    pieces = [held[d, e] for d in range(q_local) for e in range(plane)]
    chi = lax.dynamic_index_in_dim(bubble, group, 1, keepdims=False)
    place = jnp.stack([group, member]).astype(jnp.int32)
    results = ladder(place, chi, pieces, q_local, plane)
    returned = [results[0]] + [swap(results[d], d * plane) for d in range(1, q_local)]

    def device_of(global_rows):
        return global_rows // col_count // q_local * ka_count + global_rows % col_count // row_count

    def chosen_of(by_device):
        mine = (device_of(by_device) == my_device).astype(jnp.int32)
        rank = jnp.cumsum(mine, 1) - 1
        source_q = by_device // col_count % q_local
        source_place = (source_q ^ group) * row_count + by_device % col_count % row_count
        slot_ids = jnp.arange(per_peer, dtype=jnp.int32)
        hits = mine[:, :, None] * (rank[:, :, None] == slot_ids[None, None, :]).astype(jnp.int32)
        return jnp.sum(hits * source_place[:, :, None], 1)

    def slots_of(by_device):
        source_dev = device_of(
            lax.dynamic_index_in_dim(by_device, my_device, 0, keepdims=False)
        )
        onehot = (source_dev[:, None] == jnp.arange(dev_count, dtype=jnp.int32)[None, :]).astype(
            jnp.int32
        )
        slot_index = jnp.sum((jnp.cumsum(onehot, 0) - onehot) * onehot, 1)
        return source_dev, slot_index

    tables = [
        row_maps[channel]
        .reshape(pb_count, q_local, ka_count, row_count)
        .transpose(0, 2, 1, 3)
        .reshape(dev_count, local_count)
        for channel in range(2)
    ]
    chosen = jnp.stack([chosen_of(table) for table in tables], 1).reshape(-1)
    chosen = (chosen[:, None] == jnp.arange(local_count, dtype=jnp.int32)[None, :]).astype(
        jnp.bfloat16
    )
    send = select_rows(chosen, returned)
    received = lax.all_to_all(
        send.reshape(dev_count, 2 * per_peer, 2 * col_count), ("pb", "ka"), 0, 0, tiled=True
    ).reshape(dev_count * 2 * per_peer, 2 * col_count)

    stacked = jnp.stack(returned)
    order = jnp.arange(q_local, dtype=jnp.int32) ^ group
    reducible = jnp.take(stacked, order, axis=0).astype(jnp.float32)
    ladder_out = vertex_ladder + jnp.moveaxis(reducible, 0, 1)

    crossed = []
    for channel, base in ((0, vertex_cross_a), (1, vertex_cross_b)):
        source_dev, slot_index = slots_of(tables[channel])
        slot = (source_dev * 2 + channel) * per_peer + slot_index
        row_pick = (
            slot[:, None] == jnp.arange(dev_count * 2 * per_peer, dtype=jnp.int32)[None, :]
        ).astype(jnp.bfloat16)
        column_pick = (
            jnp.arange(col_count, dtype=jnp.int32)[:, None] == col_maps[channel][None, :]
        ).astype(jnp.bfloat16)
        placed = place_rows(row_pick, column_pick, received, base.reshape(2, local_count, col_count))
        crossed.append(placed.reshape(base.shape))
    return (ladder_out, crossed[0], crossed[1])


def solution(mesh):
    spread = P(None, "pb", "ka", None)
    return jax.shard_map(
        per_device,
        mesh=mesh,
        in_specs=(spread, spread, spread, P(None, "pb", None), P(), P()),
        out_specs=(spread, spread, spread),
        check_vma=False,
    )
```

```python
import functools

import jax
import jax.numpy as jnp
from jax import lax
from jax.experimental import pallas as pl
from jax.experimental.pallas import tpu as pltpu
from jax.sharding import PartitionSpec as P


LADDER = 6
TILE = 256


def ladder_kernel(groups, low_count, wanted, place_ref, chi_ref, *refs):
    total = groups * low_count * 2
    pieces = refs[:total]
    outs = refs[total : total + len(wanted)]
    right, left, base, sems = refs[total + len(wanted) :]
    rows = pieces[0].shape[1]
    depth = pieces[0].shape[2]
    count = len(wanted) * rows
    plane = 2 * low_count
    group, low, core = place_ref[0], place_ref[1], place_ref[2]

    def start_of(d, e, c):
        member = lax.bitwise_xor(core, c) * low_count + lax.bitwise_xor(low, e)
        return pl.multiple_of((lax.bitwise_xor(group, d) * plane + member) * rows, rows)

    copies = []
    for d in range(groups):
        for e in range(low_count):
            for c in range(2):
                number = (d * low_count + e) * 2 + c
                for part in range(2):
                    copy = pltpu.make_async_copy(
                        pieces[number].at[part],
                        right.at[pl.ds(part * depth + start_of(d, e, c), rows), :],
                        sems.at[number * 2 + part],
                    )
                    copy.start()
                    copies.append(copy)
    for copy in copies:
        copy.wait()
    for i, d in enumerate(wanted):
        for part in range(2):
            base[pl.ds(part * count + i * rows, rows), :] = right[
                pl.ds(part * depth + start_of(d, 0, 0), rows), :
            ]

    def scaled(slot, columns, real, imag):
        chi_re, chi_im = chi_ref[0:1, columns], chi_ref[1:2, columns]
        scaled_re = real * chi_re - imag * chi_im
        scaled_im = real * chi_im + imag * chi_re
        low_re = scaled_re.astype(jnp.bfloat16)
        low_im = scaled_im.astype(jnp.bfloat16)
        shifted = slice(columns.start + depth, columns.stop + depth)
        left[slot, :count, columns] = low_re
        left[slot, count:, columns] = low_im
        left[slot, count:, shifted] = low_re
        left[slot, :count, shifted] = -low_im

    tiles = [slice(j * TILE, (j + 1) * TILE) for j in range(depth // TILE)]
    for columns in tiles:
        whole = base[:, columns].astype(jnp.float32)
        scaled(0, columns, whole[:count], whole[count:])
    for step in range(LADDER):
        for columns in tiles:
            product = jnp.dot(
                left[step % 2], right[:, columns], preferred_element_type=jnp.float32
            )
            if step < LADDER - 1:
                whole = product + base[:, columns].astype(jnp.float32)
                scaled((step + 1) % 2, columns, whole[:count], whole[count:])
            else:
                rounded = product.astype(jnp.bfloat16)
                for i in range(len(wanted)):
                    for part in range(2):
                        start = part * count + i * rows
                        outs[i][part, :, columns] = rounded[start : start + rows]


def ladder(place, chi, pieces, groups, low_count, wanted):
    _, rows, depth = pieces[0].shape
    count = len(wanted) * rows
    total = groups * low_count * 2
    return pl.pallas_call(
        functools.partial(ladder_kernel, groups, low_count, wanted),
        out_shape=[jax.ShapeDtypeStruct((2, rows, depth), jnp.bfloat16)] * len(wanted),
        in_specs=[
            pl.BlockSpec(memory_space=pltpu.SMEM),
            pl.BlockSpec(memory_space=pltpu.VMEM),
        ]
        + [pl.BlockSpec(memory_space=pl.ANY)] * total,
        out_specs=[pl.BlockSpec(memory_space=pltpu.VMEM)] * len(wanted),
        scratch_shapes=[
            pltpu.VMEM((2 * depth, depth), jnp.bfloat16),
            pltpu.VMEM((2, 2 * count, 2 * depth), jnp.bfloat16),
            pltpu.VMEM((2 * count, depth), jnp.bfloat16),
            pltpu.SemaphoreType.DMA((total * 2,)),
        ],
        cost_estimate=pl.CostEstimate(
            flops=LADDER * 8 * count * depth * depth,
            bytes_accessed=4 * depth * depth + 8 * count * depth,
            transcendentals=0,
        ),
        name="ladder",
    )(place, chi, *pieces)


def select_kernel(chosen_ref, *refs):
    groups = len(refs) - 1
    out = refs[-1]
    depth = refs[0].shape[2]
    for part in range(2):
        rows = jnp.concatenate([refs[d][part] for d in range(groups)], 0)
        out[:, part * depth : (part + 1) * depth] = jnp.dot(
            chosen_ref[...], rows, preferred_element_type=jnp.float32
        ).astype(jnp.bfloat16)


def select_rows(chosen, returned):
    _, _, depth = returned[0].shape
    return pl.pallas_call(
        select_kernel,
        out_shape=jax.ShapeDtypeStruct((chosen.shape[0], 2 * depth), jnp.bfloat16),
        cost_estimate=pl.CostEstimate(
            flops=4 * chosen.shape[0] * chosen.shape[1] * depth,
            bytes_accessed=8 * chosen.shape[0] * depth,
            transcendentals=0,
        ),
        name="select_rows",
    )(chosen, *returned)


def place_kernel(rows_ref, columns_ref, received_ref, base_ref, out_ref):
    picked = jnp.dot(
        rows_ref[...], received_ref[...], preferred_element_type=jnp.float32
    ).astype(jnp.bfloat16)
    out_ref[0] = base_ref[0] + jnp.dot(
        picked, columns_ref[...], preferred_element_type=jnp.float32
    )


def place_rows(row_pick, column_pick, received, base):
    count, slots = row_pick.shape
    depth = column_pick.shape[0]
    return pl.pallas_call(
        place_kernel,
        out_shape=jax.ShapeDtypeStruct((2, count, depth), jnp.float32),
        grid=(2,),
        in_specs=[
            pl.BlockSpec((count, slots), lambda part: (0, 0)),
            pl.BlockSpec((depth, depth), lambda part: (0, 0)),
            pl.BlockSpec((slots, depth), lambda part: (0, part)),
            pl.BlockSpec((1, count, depth), lambda part: (part, 0, 0)),
        ],
        out_specs=pl.BlockSpec((1, count, depth), lambda part: (part, 0, 0)),
        cost_estimate=pl.CostEstimate(
            flops=4 * count * depth * (slots + depth),
            bytes_accessed=16 * count * depth + 2 * depth * depth,
            transcendentals=0,
        ),
        name="place_rows",
    )(row_pick, column_pick, received, base)


def per_device(vertex_ladder, vertex_cross_a, vertex_cross_b, bubble, row_maps, col_maps):
    _, q_local, row_count, col_count = vertex_ladder.shape
    pb_count = lax.axis_size("pb")
    ka_count = lax.axis_size("ka")
    dev_count = pb_count * ka_count
    plane = ka_count // q_local
    low_count = plane // 2
    local_count = q_local * row_count
    per_peer = local_count // dev_count
    my_pb = lax.axis_index("pb")
    my_ka = lax.axis_index("ka")
    group, member = my_ka // plane, my_ka % plane
    core, top, low = my_pb % 2, member // low_count, member % low_count

    def twin_of(index):
        pb, ka = index // ka_count, index % ka_count
        other, upper = pb % 2, ka % plane // low_count
        return (pb - other + upper) * ka_count + ka + (other - upper) * low_count

    my_device = my_pb * ka_count + my_ka
    my_twin = twin_of(my_device)

    def move(value, target):
        return lax.ppermute(value, ("pb", "ka"), [(i, target(i)) for i in range(dev_count)])

    gamma_low = vertex_ladder.astype(jnp.bfloat16)

    def piece_of(index):
        return lax.dynamic_index_in_dim(gamma_low, index, 1, keepdims=False)

    held = {}
    for d in range(q_local):
        held[d, 0, 0] = move(piece_of(group ^ d), lambda i, d=d: twin_of(i) ^ (d * plane))
    bits = [1 << b for b in range(low_count.bit_length() - 1)]
    for d in range(q_local):
        have = [0]
        for bit in bits:
            for e in have:
                held[d, e ^ bit, 0] = move(held[d, e, 0], lambda i, bit=bit: i ^ bit)
            have = have + [e ^ bit for e in have]
        for e in have:
            held[d, e, 1] = move(held[d, e, 0], lambda i: i ^ ka_count)
    pieces = [held[d, e, c] for d in range(q_local) for e in range(low_count) for c in range(2)]
    own_chi = lax.dynamic_index_in_dim(bubble, group, 1, keepdims=False)
    other_chi = move(own_chi, lambda i: i ^ ka_count)
    chi = jnp.where(core == top, own_chi, other_chi)
    place = jnp.stack([group, low, core]).astype(jnp.int32)
    results = {}
    for wanted in parts_of(q_local):
        outs = ladder(place, chi, pieces, q_local, low_count, wanted)
        for d, out in zip(wanted, outs):
            results[d] = out
    returned = [results[0]] + [
        move(results[d], lambda i, d=d: i ^ (d * plane)) for d in range(1, q_local)
    ]

    def device_of(global_rows):
        return global_rows // col_count // q_local * ka_count + global_rows % col_count // row_count

    def chosen_of(by_device):
        mine = (device_of(by_device) == my_twin).astype(jnp.int32)
        rank = jnp.cumsum(mine, 1) - 1
        source_q = by_device // col_count % q_local
        source_place = (source_q ^ group) * row_count + by_device % col_count % row_count
        slot_ids = jnp.arange(per_peer, dtype=jnp.int32)
        hits = mine[:, :, None] * (rank[:, :, None] == slot_ids[None, None, :]).astype(jnp.int32)
        return jnp.sum(hits * source_place[:, :, None], 1)

    def slots_of(by_device):
        source_dev = device_of(
            lax.dynamic_index_in_dim(by_device, my_device, 0, keepdims=False)
        )
        onehot = (source_dev[:, None] == jnp.arange(dev_count, dtype=jnp.int32)[None, :]).astype(
            jnp.int32
        )
        slot_index = jnp.sum((jnp.cumsum(onehot, 0) - onehot) * onehot, 1)
        return twin_of(source_dev), slot_index

    tables = [
        row_maps[channel]
        .reshape(pb_count, q_local, ka_count, row_count)
        .transpose(0, 2, 1, 3)
        .reshape(dev_count, local_count)
        for channel in range(2)
    ]
    chosen = jnp.stack([chosen_of(table) for table in tables], 1).reshape(-1)
    chosen = (chosen[:, None] == jnp.arange(local_count, dtype=jnp.int32)[None, :]).astype(
        jnp.bfloat16
    )
    send = select_rows(chosen, returned)
    received = lax.all_to_all(
        send.reshape(dev_count, 2 * per_peer, 2 * col_count), ("pb", "ka"), 0, 0, tiled=True
    ).reshape(dev_count * 2 * per_peer, 2 * col_count)

    stacked = jnp.stack([move(returned[d], twin_of) for d in range(q_local)])
    order = jnp.arange(q_local, dtype=jnp.int32) ^ group
    reducible = jnp.take(stacked, order, axis=0).astype(jnp.float32)
    ladder_out = vertex_ladder + jnp.moveaxis(reducible, 0, 1)

    crossed = []
    for channel, base in ((0, vertex_cross_a), (1, vertex_cross_b)):
        source_dev, slot_index = slots_of(tables[channel])
        slot = (source_dev * 2 + channel) * per_peer + slot_index
        row_pick = (
            slot[:, None] == jnp.arange(dev_count * 2 * per_peer, dtype=jnp.int32)[None, :]
        ).astype(jnp.bfloat16)
        column_pick = (
            jnp.arange(col_count, dtype=jnp.int32)[:, None] == col_maps[channel][None, :]
        ).astype(jnp.bfloat16)
        placed = place_rows(row_pick, column_pick, received, base.reshape(2, local_count, col_count))
        crossed.append(placed.reshape(base.shape))
    return (ladder_out, crossed[0], crossed[1])


def parts_of(q_local):
    return [tuple(range(q_local - 1, q_local // 2 - 1, -1)), tuple(range(q_local // 2 - 1, -1, -1))]


def solution(mesh):
    spread = P(None, "pb", "ka", None)

    return jax.shard_map(
        per_device,
        mesh=mesh,
        in_specs=(spread, spread, spread, P(None, "pb", None), P(), P()),
        out_specs=(spread, spread, spread),
        check_vma=False,
    )
```

```python
import functools

import jax
import jax.numpy as jnp
from jax import lax
from jax.experimental import pallas as pl
from jax.experimental.pallas import tpu as pltpu
from jax.sharding import PartitionSpec as P


LADDER = 6
TILE = 256
MIB = 1 << 20
SELECT_VMEM = 14 * MIB


def ladder_kernel(groups, low_count, wanted, place_ref, chi_ref, *refs):
    total = groups * low_count * 2
    pieces = refs[:total]
    outs = refs[total : total + len(wanted)]
    right, left, base, sems = refs[total + len(wanted) :]
    rows = pieces[0].shape[1]
    depth = pieces[0].shape[2]
    count = len(wanted) * rows
    plane = 2 * low_count
    group, low, core = place_ref[0], place_ref[1], place_ref[2]

    def start_of(d, e, c):
        member = lax.bitwise_xor(core, c) * low_count + lax.bitwise_xor(low, e)
        return pl.multiple_of((lax.bitwise_xor(group, d) * plane + member) * rows, rows)

    copies = []
    for d in range(groups):
        for e in range(low_count):
            for c in range(2):
                number = (d * low_count + e) * 2 + c
                for part in range(2):
                    copy = pltpu.make_async_copy(
                        pieces[number].at[part],
                        right.at[pl.ds(part * depth + start_of(d, e, c), rows), :],
                        sems.at[number * 2 + part],
                    )
                    copy.start()
                    copies.append(copy)
    for copy in copies:
        copy.wait()
    for i, d in enumerate(wanted):
        for part in range(2):
            base[pl.ds(part * count + i * rows, rows), :] = right[
                pl.ds(part * depth + start_of(d, 0, 0), rows), :
            ]

    def scaled(slot, columns, real, imag):
        chi_re, chi_im = chi_ref[0:1, columns], chi_ref[1:2, columns]
        scaled_re = real * chi_re - imag * chi_im
        scaled_im = real * chi_im + imag * chi_re
        low_re = scaled_re.astype(jnp.bfloat16)
        low_im = scaled_im.astype(jnp.bfloat16)
        shifted = slice(columns.start + depth, columns.stop + depth)
        left[slot, :count, columns] = low_re
        left[slot, count:, columns] = low_im
        left[slot, count:, shifted] = low_re
        left[slot, :count, shifted] = -low_im

    tiles = [slice(j * TILE, (j + 1) * TILE) for j in range(depth // TILE)]
    for columns in tiles:
        whole = base[:, columns].astype(jnp.float32)
        scaled(0, columns, whole[:count], whole[count:])
    for step in range(LADDER):
        for columns in tiles:
            product = jnp.dot(
                left[step % 2], right[:, columns], preferred_element_type=jnp.float32
            )
            if step < LADDER - 1:
                whole = product + base[:, columns].astype(jnp.float32)
                scaled((step + 1) % 2, columns, whole[:count], whole[count:])
            else:
                rounded = product.astype(jnp.bfloat16)
                for i in range(len(wanted)):
                    for part in range(2):
                        start = part * count + i * rows
                        outs[i][part, :, columns] = rounded[start : start + rows]


def ladder(place, chi, pieces, groups, low_count, wanted):
    _, rows, depth = pieces[0].shape
    count = len(wanted) * rows
    total = groups * low_count * 2
    return pl.pallas_call(
        functools.partial(ladder_kernel, groups, low_count, wanted),
        out_shape=[jax.ShapeDtypeStruct((2, rows, depth), jnp.bfloat16)] * len(wanted),
        in_specs=[
            pl.BlockSpec(memory_space=pltpu.SMEM),
            pl.BlockSpec(memory_space=pltpu.VMEM),
        ]
        + [pl.BlockSpec(memory_space=pl.ANY)] * total,
        out_specs=[pl.BlockSpec(memory_space=pltpu.VMEM)] * len(wanted),
        scratch_shapes=[
            pltpu.VMEM((2 * depth, depth), jnp.bfloat16),
            pltpu.VMEM((2, 2 * count, 2 * depth), jnp.bfloat16),
            pltpu.VMEM((2 * count, depth), jnp.bfloat16),
            pltpu.SemaphoreType.DMA((total * 2,)),
        ],
        cost_estimate=pl.CostEstimate(
            flops=LADDER * 8 * count * depth * depth,
            bytes_accessed=4 * depth * depth + 8 * count * depth,
            transcendentals=0,
        ),
        name="ladder",
    )(place, chi, *pieces)


def select_kernel(chosen_ref, *refs):
    groups = len(refs) - 1
    out = refs[-1]
    depth = refs[0].shape[2]
    for part in range(2):
        rows = jnp.concatenate([refs[d][part] for d in range(groups)], 0)
        out[:, part * depth : (part + 1) * depth] = jnp.dot(
            chosen_ref[...], rows, preferred_element_type=jnp.float32
        ).astype(jnp.bfloat16)


def select_rows(chosen, returned):
    _, _, depth = returned[0].shape
    return pl.pallas_call(
        select_kernel,
        out_shape=jax.ShapeDtypeStruct((chosen.shape[0], 2 * depth), jnp.bfloat16),
        cost_estimate=pl.CostEstimate(
            flops=4 * chosen.shape[0] * chosen.shape[1] * depth,
            bytes_accessed=8 * chosen.shape[0] * depth,
            transcendentals=0,
        ),
        compiler_params=pltpu.CompilerParams(vmem_limit_bytes=SELECT_VMEM),
        name="select_rows",
    )(chosen, *returned)


def place_kernel(maps_ref, rows_ref, received_ref, base_a, base_b, out_a, out_b, columns):
    depth = columns.shape[1]

    @pl.when((pl.program_id(0) == 0) & (pl.program_id(1) == 0))
    def _():
        wide = lax.broadcasted_iota(jnp.int32, (depth, depth), 0)
        for channel in range(2):
            hit = wide == maps_ref[channel : channel + 1, :]
            columns[channel] = jnp.where(hit, 1.0, 0.0).astype(jnp.bfloat16)

    for channel, (base, out) in enumerate(((base_a, out_a), (base_b, out_b))):
        picked = jnp.dot(
            rows_ref[channel], received_ref[...], preferred_element_type=jnp.float32
        ).astype(jnp.bfloat16)
        out[0] = base[0] + jnp.dot(picked, columns[channel], preferred_element_type=jnp.float32)


def place_rows(col_maps, row_pick, received, base_a, base_b):
    _, count, slots = row_pick.shape
    depth = col_maps.shape[1]
    block = pl.BlockSpec((1, count // 2, depth), lambda part, half: (part, half, 0))
    return pl.pallas_call(
        place_kernel,
        out_shape=[jax.ShapeDtypeStruct((2, count, depth), jnp.float32)] * 2,
        grid=(2, 2),
        in_specs=[
            pl.BlockSpec((2, depth), lambda part, half: (0, 0)),
            pl.BlockSpec((2, count // 2, slots), lambda part, half: (0, half, 0)),
            pl.BlockSpec((slots, depth), lambda part, half: (0, part)),
            block,
            block,
        ],
        out_specs=[block, block],
        scratch_shapes=[pltpu.VMEM((2, depth, depth), jnp.bfloat16)],
        cost_estimate=pl.CostEstimate(
            flops=8 * count * depth * (slots + depth),
            bytes_accessed=32 * count * depth,
            transcendentals=0,
        ),
        name="place_rows",
    )(col_maps, row_pick, received, base_a, base_b)


def per_device(vertex_ladder, vertex_cross_a, vertex_cross_b, bubble, row_maps, col_maps):
    _, q_local, row_count, col_count = vertex_ladder.shape
    pb_count = lax.axis_size("pb")
    ka_count = lax.axis_size("ka")
    dev_count = pb_count * ka_count
    plane = ka_count // q_local
    low_count = plane // 2
    local_count = q_local * row_count
    per_peer = local_count // dev_count
    my_pb = lax.axis_index("pb")
    my_ka = lax.axis_index("ka")
    group, member = my_ka // plane, my_ka % plane
    core, top, low = my_pb % 2, member // low_count, member % low_count

    def twin_of(index):
        pb, ka = index // ka_count, index % ka_count
        other, upper = pb % 2, ka % plane // low_count
        return (pb - other + upper) * ka_count + ka + (other - upper) * low_count

    my_device = my_pb * ka_count + my_ka
    my_twin = twin_of(my_device)

    def move(value, target):
        return lax.ppermute(value, ("pb", "ka"), [(i, target(i)) for i in range(dev_count)])

    def piece_of(index):
        piece = lax.dynamic_index_in_dim(vertex_ladder, index, 1, keepdims=False)
        return piece.astype(jnp.bfloat16)

    held = {}
    for d in range(q_local):
        held[d, 0, 0] = move(piece_of(group ^ d), lambda i, d=d: twin_of(i) ^ (d * plane))
    bits = [1 << b for b in range(low_count.bit_length() - 1)]
    for d in range(q_local):
        have = [0]
        for bit in bits:
            for e in have:
                held[d, e ^ bit, 0] = move(held[d, e, 0], lambda i, bit=bit: i ^ bit)
            have = have + [e ^ bit for e in have]
        for e in have:
            held[d, e, 1] = move(held[d, e, 0], lambda i: i ^ ka_count)
    pieces = [held[d, e, c] for d in range(q_local) for e in range(low_count) for c in range(2)]
    own_chi = lax.dynamic_index_in_dim(bubble, group, 1, keepdims=False)
    other_chi = move(own_chi, lambda i: i ^ ka_count)
    chi = jnp.where(core == top, own_chi, other_chi)
    place = jnp.stack([group, low, core]).astype(jnp.int32)
    results = {}
    for wanted in parts_of(q_local):
        outs = ladder(place, chi, pieces, q_local, low_count, wanted)
        for d, out in zip(wanted, outs):
            results[d] = out
    returned = [results[0]] + [
        move(results[d], lambda i, d=d: i ^ (d * plane)) for d in range(1, q_local)
    ]

    def device_of(global_rows):
        return global_rows // col_count // q_local * ka_count + global_rows % col_count // row_count

    def chosen_of(by_device):
        mine = (device_of(by_device) == my_twin).astype(jnp.int32)
        rank = jnp.cumsum(mine, 1) - 1
        source_q = by_device // col_count % q_local
        source_place = (source_q ^ group) * row_count + by_device % col_count % row_count
        slot_ids = jnp.arange(per_peer, dtype=jnp.int32)
        hits = mine[:, :, None] * (rank[:, :, None] == slot_ids[None, None, :]).astype(jnp.int32)
        return jnp.sum(hits * source_place[:, :, None], 1)

    def slots_of(by_device):
        source_dev = device_of(
            lax.dynamic_index_in_dim(by_device, my_device, 0, keepdims=False)
        )
        onehot = (source_dev[:, None] == jnp.arange(dev_count, dtype=jnp.int32)[None, :]).astype(
            jnp.int32
        )
        slot_index = jnp.sum((jnp.cumsum(onehot, 0) - onehot) * onehot, 1)
        return twin_of(source_dev), slot_index

    tables = [
        row_maps[channel]
        .reshape(pb_count, q_local, ka_count, row_count)
        .transpose(0, 2, 1, 3)
        .reshape(dev_count, local_count)
        for channel in range(2)
    ]
    chosen = jnp.stack([chosen_of(table) for table in tables], 1).reshape(-1)
    chosen = (chosen[:, None] == jnp.arange(local_count, dtype=jnp.int32)[None, :]).astype(
        jnp.bfloat16
    )
    send = select_rows(chosen, returned)
    received = lax.all_to_all(
        send.reshape(dev_count, 2 * per_peer, 2 * col_count), ("pb", "ka"), 0, 0, tiled=True
    ).reshape(dev_count * 2 * per_peer, 2 * col_count)

    stacked = jnp.stack([move(returned[d], twin_of) for d in range(q_local)])
    order = jnp.arange(q_local, dtype=jnp.int32) ^ group
    reducible = jnp.take(stacked, order, axis=0).astype(jnp.float32)
    ladder_out = vertex_ladder + jnp.moveaxis(reducible, 0, 1)

    row_pick = []
    for channel in range(2):
        source_dev, slot_index = slots_of(tables[channel])
        slot = (source_dev * 2 + channel) * per_peer + slot_index
        row_pick.append(slot[:, None] == jnp.arange(dev_count * 2 * per_peer, dtype=jnp.int32))
    crossed_a, crossed_b = place_rows(
        col_maps,
        jnp.stack(row_pick).astype(jnp.bfloat16),
        received,
        vertex_cross_a.reshape(2, local_count, col_count),
        vertex_cross_b.reshape(2, local_count, col_count),
    )
    return (
        ladder_out,
        crossed_a.reshape(vertex_cross_a.shape),
        crossed_b.reshape(vertex_cross_b.shape),
    )


def parts_of(q_local):
    return [tuple(range(q_local - 1, q_local // 2 - 1, -1)), tuple(range(q_local // 2 - 1, -1, -1))]


def solution(mesh):
    spread = P(None, "pb", "ka", None)

    return jax.shard_map(
        per_device,
        mesh=mesh,
        in_specs=(spread, spread, spread, P(None, "pb", None), P(), P()),
        out_specs=(spread, spread, spread),
        check_vma=False,
    )
```

```python
import functools

import jax
import jax.numpy as jnp
from jax import lax
from jax.experimental import pallas as pl
from jax.experimental.pallas import tpu as pltpu
from jax.sharding import PartitionSpec as P


LADDER = 6
TILE = 256
MIB = 1 << 20
LADDER_VMEM = 20 * MIB
TOTAL_VMEM = 10 * MIB
SELECT_VMEM = 14 * MIB


def ladder_steps(groups, low_count, wanted, place_ref, chi_ref, right, outs, left, base):
    depth = right.shape[1]
    rows = depth // (groups * low_count * 2)
    count = len(wanted) * rows
    for i, d in enumerate(wanted):
        start = start_of(low_count, rows, place_ref, d, 0, 0)
        for part in range(2):
            base[pl.ds(part * count + i * rows, rows), :] = right[
                pl.ds(part * depth + start, rows), :
            ]

    def scaled(slot, columns, real, imag):
        chi_re, chi_im = chi_ref[0:1, columns], chi_ref[1:2, columns]
        scaled_re = real * chi_re - imag * chi_im
        scaled_im = real * chi_im + imag * chi_re
        low_re = scaled_re.astype(jnp.bfloat16)
        low_im = scaled_im.astype(jnp.bfloat16)
        shifted = slice(columns.start + depth, columns.stop + depth)
        left[slot, :count, columns] = low_re
        left[slot, count:, columns] = low_im
        left[slot, count:, shifted] = low_re
        left[slot, :count, shifted] = -low_im

    tiles = [slice(j * TILE, (j + 1) * TILE) for j in range(depth // TILE)]
    for columns in tiles:
        whole = base[:, columns].astype(jnp.float32)
        scaled(0, columns, whole[:count], whole[count:])
    for step in range(LADDER):
        for columns in tiles:
            product = jnp.dot(
                left[step % 2], right[:, columns], preferred_element_type=jnp.float32
            )
            if step < LADDER - 1:
                whole = product + base[:, columns].astype(jnp.float32)
                scaled((step + 1) % 2, columns, whole[:count], whole[count:])
            else:
                rounded = product.astype(jnp.bfloat16)
                for i in range(len(wanted)):
                    for part in range(2):
                        start = part * count + i * rows
                        outs[i][part, :, columns] = rounded[start : start + rows]


def start_of(low_count, rows, place_ref, d, e, c):
    member = lax.bitwise_xor(place_ref[2], c) * low_count + lax.bitwise_xor(place_ref[1], e)
    return pl.multiple_of(
        (lax.bitwise_xor(place_ref[0], d) * 2 * low_count + member) * rows, rows
    )


def first_kernel(groups, low_count, wanted, place_ref, chi_ref, *refs):
    total = groups * low_count * 2
    pieces = refs[:total]
    outs = refs[total : total + len(wanted)]
    right, left, base = refs[total + len(wanted) :]
    rows, depth = pieces[0].shape[1:]
    for d in range(groups):
        for e in range(low_count):
            for c in range(2):
                piece = pieces[(d * low_count + e) * 2 + c]
                start = start_of(low_count, rows, place_ref, d, e, c)
                for part in range(2):
                    right[pl.ds(part * depth + start, rows), :] = piece[part]
    ladder_steps(groups, low_count, wanted, place_ref, chi_ref, right, outs, left, base)


def next_kernel(groups, low_count, wanted, place_ref, chi_ref, right, *refs):
    outs = refs[: len(wanted)]
    left, base = refs[len(wanted) :]
    ladder_steps(groups, low_count, wanted, place_ref, chi_ref, right, outs, left, base)


def ladder(place, chi, pieces, right, groups, low_count, wanted):
    _, rows, depth = pieces[0].shape
    count = len(wanted) * rows
    total = groups * low_count * 2
    vmem = pl.BlockSpec(memory_space=pltpu.VMEM)
    first = right is None
    shapes = [jax.ShapeDtypeStruct((2, rows, depth), jnp.bfloat16)] * len(wanted)
    if first:
        shapes.append(jax.ShapeDtypeStruct((2 * depth, depth), jnp.bfloat16))
    return pl.pallas_call(
        functools.partial(first_kernel if first else next_kernel, groups, low_count, wanted),
        out_shape=shapes,
        in_specs=[pl.BlockSpec(memory_space=pltpu.SMEM), vmem]
        + [vmem] * (total if first else 1),
        out_specs=[vmem] * len(shapes),
        scratch_shapes=[
            pltpu.VMEM((2, 2 * count, 2 * depth), jnp.bfloat16),
            pltpu.VMEM((2 * count, depth), jnp.bfloat16),
        ],
        cost_estimate=pl.CostEstimate(
            flops=LADDER * 8 * count * depth * depth,
            bytes_accessed=4 * depth * depth * first + 8 * count * depth,
            transcendentals=0,
        ),
        compiler_params=pltpu.CompilerParams(vmem_limit_bytes=LADDER_VMEM),
        name="ladder",
    )(place, chi, *(pieces if first else [right]))


def select_kernel(chosen_ref, *refs):
    groups = len(refs) - 1
    out = refs[-1]
    depth = refs[0].shape[2]
    for part in range(2):
        rows = jnp.concatenate([refs[d][part] for d in range(groups)], 0)
        for channel in range(2):
            start = (channel * 2 + part) * depth
            out[:, start : start + depth] = jnp.dot(
                chosen_ref[channel], rows, preferred_element_type=jnp.float32
            ).astype(jnp.bfloat16)


def select_rows(chosen, returned):
    _, _, depth = returned[0].shape
    _, slots, count = chosen.shape
    return pl.pallas_call(
        select_kernel,
        out_shape=jax.ShapeDtypeStruct((slots, 4 * depth), jnp.bfloat16),
        cost_estimate=pl.CostEstimate(
            flops=8 * slots * count * depth,
            bytes_accessed=16 * slots * depth,
            transcendentals=0,
        ),
        compiler_params=pltpu.CompilerParams(vmem_limit_bytes=SELECT_VMEM),
        name="select_rows",
    )(chosen, *returned)


def place_kernel(maps_ref, rows_ref, got, base_a, base_b, out_a, out_b, *scratch):
    columns, base, moved, in_sems, out_sems = scratch
    depth = columns.shape[1]
    bases, outs = (base_a, base_b), (out_a, out_b)
    arriving, leaving = {}, []
    for channel in range(2):
        for part in range(2):
            copy = pltpu.make_async_copy(
                bases[channel].at[part], base.at[channel, part], in_sems.at[channel, part]
            )
            copy.start()
            arriving[channel, part] = copy
    wide = lax.broadcasted_iota(jnp.int32, (depth, depth), 0)
    for channel in range(2):
        hit = wide == maps_ref[channel : channel + 1, :]
        columns[channel] = jnp.where(hit, 1.0, 0.0).astype(jnp.bfloat16)
    for channel in range(2):
        for part in range(2):
            start = (channel * 2 + part) * depth
            picked = jnp.dot(
                rows_ref[channel],
                got[:, start : start + depth],
                preferred_element_type=jnp.float32,
            ).astype(jnp.bfloat16)
            arriving[channel, part].wait()
            moved[channel, part] = base[channel, part] + jnp.dot(
                picked, columns[channel], preferred_element_type=jnp.float32
            )
            copy = pltpu.make_async_copy(
                moved.at[channel, part], outs[channel].at[part], out_sems.at[channel, part]
            )
            copy.start()
            leaving.append(copy)
    for copy in leaving:
        copy.wait()


def place_rows(col_maps, row_pick, received, base_a, base_b):
    _, count, slots = row_pick.shape
    depth = col_maps.shape[1]
    vmem, hbm = pl.BlockSpec(memory_space=pltpu.VMEM), pl.BlockSpec(memory_space=pltpu.HBM)
    return pl.pallas_call(
        place_kernel,
        out_shape=[jax.ShapeDtypeStruct((2, count, depth), jnp.float32)] * 2,
        in_specs=[vmem, vmem, vmem, hbm, hbm],
        out_specs=[hbm, hbm],
        scratch_shapes=[
            pltpu.VMEM((2, depth, depth), jnp.bfloat16),
            pltpu.VMEM((2, 2, count, depth), jnp.float32),
            pltpu.VMEM((2, 2, count, depth), jnp.float32),
            pltpu.SemaphoreType.DMA((2, 2)),
            pltpu.SemaphoreType.DMA((2, 2)),
        ],
        cost_estimate=pl.CostEstimate(
            flops=8 * count * depth * (slots + depth),
            bytes_accessed=32 * count * depth,
            transcendentals=0,
        ),
        name="place_rows",
    )(col_maps, row_pick, received, base_a, base_b)


def total_kernel(groups, place_ref, vertex, *refs):
    parts, out = refs[:groups], refs[groups]
    held, in_sems, out_sems = refs[groups + 1 :]
    arriving, leaving = [], []
    for d in range(groups):
        index = lax.bitwise_xor(place_ref[0], d)
        arriving.append(
            pltpu.make_async_copy(vertex.at[:, index], held.at[0, d], in_sems.at[d])
        )
        leaving.append(pltpu.make_async_copy(held.at[1, d], out.at[:, index], out_sems.at[d]))
        arriving[d].start()
    for d in range(groups):
        arriving[d].wait()
        held[1, d] = held[0, d] + parts[d][...].astype(jnp.float32)
        leaving[d].start()
    for d in range(groups):
        leaving[d].wait()


def total(place, vertex, parts):
    groups = len(parts)
    vmem, hbm = pl.BlockSpec(memory_space=pltpu.VMEM), pl.BlockSpec(memory_space=pltpu.HBM)
    return pl.pallas_call(
        functools.partial(total_kernel, groups),
        out_shape=jax.ShapeDtypeStruct(vertex.shape, jnp.float32),
        in_specs=[pl.BlockSpec(memory_space=pltpu.SMEM), hbm] + [vmem] * groups,
        out_specs=hbm,
        scratch_shapes=[
            pltpu.VMEM((2, groups, *parts[0].shape), jnp.float32),
            pltpu.SemaphoreType.DMA((groups,)),
            pltpu.SemaphoreType.DMA((groups,)),
        ],
        cost_estimate=pl.CostEstimate(
            flops=vertex.size, bytes_accessed=10 * vertex.size, transcendentals=0
        ),
        compiler_params=pltpu.CompilerParams(vmem_limit_bytes=TOTAL_VMEM),
        name="total",
    )(place, vertex, *parts)


def per_device(vertex_ladder, vertex_cross_a, vertex_cross_b, bubble, row_maps, col_maps):
    _, q_local, row_count, col_count = vertex_ladder.shape
    pb_count = lax.axis_size("pb")
    ka_count = lax.axis_size("ka")
    dev_count = pb_count * ka_count
    plane = ka_count // q_local
    low_count = plane // 2
    local_count = q_local * row_count
    per_peer = local_count // dev_count
    my_pb = lax.axis_index("pb")
    my_ka = lax.axis_index("ka")
    group, member = my_ka // plane, my_ka % plane
    core, top, low = my_pb % 2, member // low_count, member % low_count

    def twin_of(index):
        pb, ka = index // ka_count, index % ka_count
        other, upper = pb % 2, ka % plane // low_count
        return (pb - other + upper) * ka_count + ka + (other - upper) * low_count

    my_device = my_pb * ka_count + my_ka
    my_twin = twin_of(my_device)

    def move(value, target):
        return lax.ppermute(value, ("pb", "ka"), [(i, target(i)) for i in range(dev_count)])

    def piece_of(index):
        piece = lax.dynamic_index_in_dim(vertex_ladder, index, 1, keepdims=False)
        return piece.astype(jnp.bfloat16)

    held = {}
    for d in range(q_local):
        held[d, 0, 0] = move(piece_of(group ^ d), lambda i, d=d: twin_of(i) ^ (d * plane))
    bits = [1 << b for b in range(low_count.bit_length() - 1)]
    for d in range(q_local):
        have = [0]
        for bit in bits:
            for e in have:
                held[d, e ^ bit, 0] = move(held[d, e, 0], lambda i, bit=bit: i ^ bit)
            have = have + [e ^ bit for e in have]
        for e in have:
            held[d, e, 1] = move(held[d, e, 0], lambda i: i ^ ka_count)
    pieces = [held[d, e, c] for d in range(q_local) for e in range(low_count) for c in range(2)]
    own_chi = lax.dynamic_index_in_dim(bubble, group, 1, keepdims=False)
    other_chi = move(own_chi, lambda i: i ^ ka_count)
    chi = jnp.where(core == top, own_chi, other_chi)
    place = jnp.stack([group, low, core]).astype(jnp.int32)
    results, right = {}, None
    for number, wanted in enumerate(parts_of(q_local)):
        outs = ladder(place, chi, pieces, right, q_local, low_count, wanted)
        right = outs[-1] if number == 0 else right
        for d, out in zip(wanted, outs):
            results[d] = out
    returned = [results[0]] + [
        move(results[d], lambda i, d=d: i ^ (d * plane)) for d in range(1, q_local)
    ]

    def device_of(global_rows):
        return global_rows // col_count // q_local * ka_count + global_rows % col_count // row_count

    def chosen_of(by_device):
        mine = (device_of(by_device) == my_twin).astype(jnp.int32)
        rank = jnp.cumsum(mine, 1) - 1
        source_q = by_device // col_count % q_local
        source_place = (source_q ^ group) * row_count + by_device % col_count % row_count
        slot_ids = jnp.arange(per_peer, dtype=jnp.int32)
        hits = mine[:, :, None] * (rank[:, :, None] == slot_ids[None, None, :]).astype(jnp.int32)
        return jnp.sum(hits * source_place[:, :, None], 1)

    def slots_of(by_device):
        source_dev = device_of(
            lax.dynamic_index_in_dim(by_device, my_device, 0, keepdims=False)
        )
        onehot = (source_dev[:, None] == jnp.arange(dev_count, dtype=jnp.int32)[None, :]).astype(
            jnp.int32
        )
        slot_index = jnp.sum((jnp.cumsum(onehot, 0) - onehot) * onehot, 1)
        return twin_of(source_dev), slot_index

    tables = [
        row_maps[channel]
        .reshape(pb_count, q_local, ka_count, row_count)
        .transpose(0, 2, 1, 3)
        .reshape(dev_count, local_count)
        for channel in range(2)
    ]
    chosen = jnp.stack([chosen_of(table) for table in tables]).reshape(2, local_count, 1)
    chosen = (chosen == jnp.arange(local_count, dtype=jnp.int32)).astype(jnp.bfloat16)
    send = select_rows(chosen, returned)
    received = lax.all_to_all(
        send.reshape(dev_count, per_peer, 4 * col_count), ("pb", "ka"), 0, 0, tiled=True
    ).reshape(local_count, 4 * col_count)

    ladder_out = total(place, vertex_ladder, [move(returned[d], twin_of) for d in range(q_local)])

    row_pick = []
    for channel in range(2):
        source_dev, slot_index = slots_of(tables[channel])
        slot = source_dev * per_peer + slot_index
        row_pick.append(slot[:, None] == jnp.arange(local_count, dtype=jnp.int32))
    crossed_a, crossed_b = place_rows(
        col_maps,
        jnp.stack(row_pick).astype(jnp.bfloat16),
        received,
        vertex_cross_a.reshape(2, local_count, col_count),
        vertex_cross_b.reshape(2, local_count, col_count),
    )
    return (
        ladder_out,
        crossed_a.reshape(vertex_cross_a.shape),
        crossed_b.reshape(vertex_cross_b.shape),
    )


def parts_of(q_local):
    return [(d,) for d in range(q_local - 1, -1, -1)]


def solution(mesh):
    spread = P(None, "pb", "ka", None)

    return jax.shard_map(
        per_device,
        mesh=mesh,
        in_specs=(spread, spread, spread, P(None, "pb", None), P(), P()),
        out_specs=(spread, spread, spread),
        check_vma=False,
    )
```

```python
import functools

import jax
import jax.numpy as jnp
from jax import lax
from jax.experimental import pallas as pl
from jax.experimental.pallas import tpu as pltpu
from jax.sharding import PartitionSpec as P


LADDER = 6
TILE = 256
MIB = 1 << 20
LADDER_VMEM = 20 * MIB
TOTAL_VMEM = 10 * MIB
SELECT_VMEM = 14 * MIB


def ladder_steps(groups, low_count, wanted, place_ref, chi_ref, right, outs, left, base):
    depth = right.shape[1]
    rows = depth // (groups * low_count * 2)
    count = len(wanted) * rows
    for i, d in enumerate(wanted):
        start = start_of(low_count, rows, place_ref, d, 0, 0)
        for part in range(2):
            base[pl.ds(part * count + i * rows, rows), :] = right[
                pl.ds(part * depth + start, rows), :
            ]

    def scaled(slot, columns, real, imag):
        chi_re, chi_im = chi_ref[0:1, columns], chi_ref[1:2, columns]
        scaled_re = real * chi_re - imag * chi_im
        scaled_im = real * chi_im + imag * chi_re
        low_re = scaled_re.astype(jnp.bfloat16)
        low_im = scaled_im.astype(jnp.bfloat16)
        shifted = slice(columns.start + depth, columns.stop + depth)
        left[slot, :count, columns] = low_re
        left[slot, count:, columns] = low_im
        left[slot, count:, shifted] = low_re
        left[slot, :count, shifted] = -low_im

    tiles = [slice(j * TILE, (j + 1) * TILE) for j in range(depth // TILE)]
    for columns in tiles:
        whole = base[:, columns].astype(jnp.float32)
        scaled(0, columns, whole[:count], whole[count:])
    for step in range(LADDER):
        for columns in tiles:
            product = jnp.dot(
                left[step % 2], right[:, columns], preferred_element_type=jnp.float32
            )
            if step < LADDER - 1:
                whole = product + base[:, columns].astype(jnp.float32)
                scaled((step + 1) % 2, columns, whole[:count], whole[count:])
            else:
                rounded = product.astype(jnp.bfloat16)
                for i in range(len(wanted)):
                    for part in range(2):
                        start = part * count + i * rows
                        outs[i][part, :, columns] = rounded[start : start + rows]


def start_of(low_count, rows, place_ref, d, e, c):
    member = lax.bitwise_xor(place_ref[2], c) * low_count + lax.bitwise_xor(place_ref[1], e)
    return pl.multiple_of(
        (lax.bitwise_xor(place_ref[0], d) * 2 * low_count + member) * rows, rows
    )


def first_kernel(groups, low_count, wanted, place_ref, chi_ref, *refs):
    total = groups * low_count * 2
    pieces = refs[:total]
    outs = refs[total : total + len(wanted)]
    right, left, base = refs[total + len(wanted) :]
    rows, depth = pieces[0].shape[1:]
    for d in range(groups):
        for e in range(low_count):
            for c in range(2):
                piece = pieces[(d * low_count + e) * 2 + c]
                start = start_of(low_count, rows, place_ref, d, e, c)
                for part in range(2):
                    right[pl.ds(part * depth + start, rows), :] = piece[part]
    ladder_steps(groups, low_count, wanted, place_ref, chi_ref, right, outs, left, base)


def next_kernel(groups, low_count, wanted, place_ref, chi_ref, right, *refs):
    outs = refs[: len(wanted)]
    left, base = refs[len(wanted) :]
    ladder_steps(groups, low_count, wanted, place_ref, chi_ref, right, outs, left, base)


def ladder(place, chi, pieces, right, groups, low_count, wanted):
    _, rows, depth = pieces[0].shape
    count = len(wanted) * rows
    total = groups * low_count * 2
    vmem = pl.BlockSpec(memory_space=pltpu.VMEM)
    first = right is None
    shapes = [jax.ShapeDtypeStruct((2, rows, depth), jnp.bfloat16)] * len(wanted)
    if first:
        shapes.append(jax.ShapeDtypeStruct((2 * depth, depth), jnp.bfloat16))
    return pl.pallas_call(
        functools.partial(first_kernel if first else next_kernel, groups, low_count, wanted),
        out_shape=shapes,
        in_specs=[pl.BlockSpec(memory_space=pltpu.SMEM), vmem]
        + [vmem] * (total if first else 1),
        out_specs=[vmem] * len(shapes),
        scratch_shapes=[
            pltpu.VMEM((2, 2 * count, 2 * depth), jnp.bfloat16),
            pltpu.VMEM((2 * count, depth), jnp.bfloat16),
        ],
        cost_estimate=pl.CostEstimate(
            flops=LADDER * 8 * count * depth * depth,
            bytes_accessed=4 * depth * depth * first + 8 * count * depth,
            transcendentals=0,
        ),
        compiler_params=pltpu.CompilerParams(vmem_limit_bytes=LADDER_VMEM),
        name="ladder",
    )(place, chi, *(pieces if first else [right]))


def select_kernel(chosen_ref, *refs):
    groups = len(refs) - 1
    out = refs[-1]
    depth = refs[0].shape[2]
    for part in range(2):
        rows = jnp.concatenate([refs[d][part] for d in range(groups)], 0)
        for channel in range(2):
            start = (channel * 2 + part) * depth
            out[:, start : start + depth] = jnp.dot(
                chosen_ref[channel], rows, preferred_element_type=jnp.float32
            ).astype(jnp.bfloat16)


def select_rows(chosen, returned):
    _, _, depth = returned[0].shape
    _, slots, count = chosen.shape
    return pl.pallas_call(
        select_kernel,
        out_shape=jax.ShapeDtypeStruct((slots, 4 * depth), jnp.bfloat16),
        cost_estimate=pl.CostEstimate(
            flops=8 * slots * count * depth,
            bytes_accessed=16 * slots * depth,
            transcendentals=0,
        ),
        compiler_params=pltpu.CompilerParams(vmem_limit_bytes=SELECT_VMEM),
        name="select_rows",
    )(chosen, *returned)


def place_kernel(maps_ref, rows_ref, received, base_a, base_b, out_a, out_b, *scratch):
    columns, got, base, moved, got_sems, in_sems, out_sems = scratch
    depth = columns.shape[1]
    bases, outs = (base_a, base_b), (out_a, out_b)
    landing, arriving, leaving = {}, {}, []
    for channel in range(2):
        for part in range(2):
            span = pl.ds((channel * 2 + part) * depth, depth)
            landing[channel, part] = pltpu.make_async_copy(
                received.at[:, span], got.at[channel, part], got_sems.at[channel, part]
            )
            arriving[channel, part] = pltpu.make_async_copy(
                bases[channel].at[part], base.at[channel, part], in_sems.at[channel, part]
            )
    turns = [(channel, part) for channel in range(2) for part in range(2)]
    for turn in turns[:2]:
        landing[turn].start()
        arriving[turn].start()
    wide = lax.broadcasted_iota(jnp.int32, (depth, depth), 0)
    for channel in range(2):
        hit = wide == maps_ref[channel : channel + 1, :]
        columns[channel] = jnp.where(hit, 1.0, 0.0).astype(jnp.bfloat16)
    for number, (channel, part) in enumerate(turns):
        landing[channel, part].wait()
        if number + 2 < len(turns):
            landing[turns[number + 2]].start()
            arriving[turns[number + 2]].start()
        picked = jnp.dot(
            rows_ref[channel], got[channel, part], preferred_element_type=jnp.float32
        ).astype(jnp.bfloat16)
        arriving[channel, part].wait()
        moved[channel, part] = base[channel, part] + jnp.dot(
            picked, columns[channel], preferred_element_type=jnp.float32
        )
        copy = pltpu.make_async_copy(
            moved.at[channel, part], outs[channel].at[part], out_sems.at[channel, part]
        )
        copy.start()
        leaving.append(copy)
    for copy in leaving:
        copy.wait()


def place_rows(col_maps, row_pick, received, base_a, base_b):
    _, count, slots = row_pick.shape
    depth = col_maps.shape[1]
    vmem, hbm = pl.BlockSpec(memory_space=pltpu.VMEM), pl.BlockSpec(memory_space=pltpu.HBM)
    return pl.pallas_call(
        place_kernel,
        out_shape=[jax.ShapeDtypeStruct((2, count, depth), jnp.float32)] * 2,
        in_specs=[vmem, vmem, hbm, hbm, hbm],
        out_specs=[hbm, hbm],
        scratch_shapes=[
            pltpu.VMEM((2, depth, depth), jnp.bfloat16),
            pltpu.VMEM((2, 2, slots, depth), jnp.bfloat16),
            pltpu.VMEM((2, 2, count, depth), jnp.float32),
            pltpu.VMEM((2, 2, count, depth), jnp.float32),
            pltpu.SemaphoreType.DMA((2, 2)),
            pltpu.SemaphoreType.DMA((2, 2)),
            pltpu.SemaphoreType.DMA((2, 2)),
        ],
        cost_estimate=pl.CostEstimate(
            flops=8 * count * depth * (slots + depth),
            bytes_accessed=32 * count * depth,
            transcendentals=0,
        ),
        name="place_rows",
    )(col_maps, row_pick, received, base_a, base_b)


def total_kernel(groups, place_ref, vertex, *refs):
    parts, out = refs[:groups], refs[groups]
    held, in_sems, out_sems = refs[groups + 1 :]
    arriving, leaving = [], []
    for d in range(groups):
        index = lax.bitwise_xor(place_ref[0], d)
        arriving.append(
            pltpu.make_async_copy(vertex.at[:, index], held.at[0, d], in_sems.at[d])
        )
        leaving.append(pltpu.make_async_copy(held.at[1, d], out.at[:, index], out_sems.at[d]))
        arriving[d].start()
    for d in range(groups):
        arriving[d].wait()
        held[1, d] = held[0, d] + parts[d][...].astype(jnp.float32)
        leaving[d].start()
    for d in range(groups):
        leaving[d].wait()


def total(place, vertex, parts):
    groups = len(parts)
    vmem, hbm = pl.BlockSpec(memory_space=pltpu.VMEM), pl.BlockSpec(memory_space=pltpu.HBM)
    return pl.pallas_call(
        functools.partial(total_kernel, groups),
        out_shape=jax.ShapeDtypeStruct(vertex.shape, jnp.float32),
        in_specs=[pl.BlockSpec(memory_space=pltpu.SMEM), hbm] + [vmem] * groups,
        out_specs=hbm,
        scratch_shapes=[
            pltpu.VMEM((2, groups, *parts[0].shape), jnp.float32),
            pltpu.SemaphoreType.DMA((groups,)),
            pltpu.SemaphoreType.DMA((groups,)),
        ],
        cost_estimate=pl.CostEstimate(
            flops=vertex.size, bytes_accessed=10 * vertex.size, transcendentals=0
        ),
        compiler_params=pltpu.CompilerParams(vmem_limit_bytes=TOTAL_VMEM),
        name="total",
    )(place, vertex, *parts)


def per_device(vertex_ladder, vertex_cross_a, vertex_cross_b, bubble, row_maps, col_maps):
    _, q_local, row_count, col_count = vertex_ladder.shape
    pb_count = lax.axis_size("pb")
    ka_count = lax.axis_size("ka")
    dev_count = pb_count * ka_count
    plane = ka_count // q_local
    low_count = plane // 2
    local_count = q_local * row_count
    per_peer = local_count // dev_count
    my_pb = lax.axis_index("pb")
    my_ka = lax.axis_index("ka")
    group, member = my_ka // plane, my_ka % plane
    core, top, low = my_pb % 2, member // low_count, member % low_count

    def twin_of(index):
        pb, ka = index // ka_count, index % ka_count
        other, upper = pb % 2, ka % plane // low_count
        return (pb - other + upper) * ka_count + ka + (other - upper) * low_count

    my_device = my_pb * ka_count + my_ka
    my_twin = twin_of(my_device)

    def move(value, target):
        return lax.ppermute(value, ("pb", "ka"), [(i, target(i)) for i in range(dev_count)])

    def piece_of(whole, index):
        piece = lax.dynamic_index_in_dim(whole, index, 1, keepdims=False)
        return piece.astype(jnp.bfloat16)

    held = {}
    first = [0, q_local - 1]
    cast = [piece_of(vertex_ladder, group ^ d) for d in first]
    *cast, whole = lax.optimization_barrier((*cast, vertex_ladder))
    cast = dict(zip(first, cast))
    for d in range(q_local):
        piece = cast[d] if d in cast else piece_of(whole, group ^ d)
        held[d, 0, 0] = move(piece, lambda i, d=d: twin_of(i) ^ (d * plane))
    bits = [1 << b for b in range(low_count.bit_length() - 1)]
    for d in range(q_local):
        have = [0]
        for bit in bits:
            for e in have:
                held[d, e ^ bit, 0] = move(held[d, e, 0], lambda i, bit=bit: i ^ bit)
            have = have + [e ^ bit for e in have]
        for e in have:
            held[d, e, 1] = move(held[d, e, 0], lambda i: i ^ ka_count)
    pieces = [held[d, e, c] for d in range(q_local) for e in range(low_count) for c in range(2)]
    own_chi = lax.dynamic_index_in_dim(bubble, group, 1, keepdims=False)
    other_chi = move(own_chi, lambda i: i ^ ka_count)
    chi = jnp.where(core == top, own_chi, other_chi)
    place = jnp.stack([group, low, core]).astype(jnp.int32)
    results, right = {}, None
    for number, wanted in enumerate(parts_of(q_local)):
        outs = ladder(place, chi, pieces, right, q_local, low_count, wanted)
        right = outs[-1] if number == 0 else right
        for d, out in zip(wanted, outs):
            results[d] = out
    returned = [results[0]] + [
        move(results[d], lambda i, d=d: i ^ (d * plane)) for d in range(1, q_local)
    ]

    def device_of(global_rows):
        return global_rows // col_count // q_local * ka_count + global_rows % col_count // row_count

    def ranks(flags, axis):
        count = jnp.arange(flags.shape[axis], dtype=jnp.int32)
        before = (count[:, None] <= count[None, :]).astype(jnp.bfloat16)
        low_flags = flags.astype(jnp.bfloat16)
        if axis == 1:
            sums = jnp.dot(low_flags, before, preferred_element_type=jnp.float32)
        else:
            sums = jnp.dot(before.T, low_flags, preferred_element_type=jnp.float32)
        return sums.astype(jnp.int32)

    def chosen_of(by_device):
        mine = (device_of(by_device) == my_twin).astype(jnp.int32)
        rank = ranks(mine, 1) - 1
        source_q = by_device // col_count % q_local
        source_place = (source_q ^ group) * row_count + by_device % col_count % row_count
        slot_ids = jnp.arange(per_peer, dtype=jnp.int32)
        hits = mine[:, :, None] * (rank[:, :, None] == slot_ids[None, None, :]).astype(jnp.int32)
        return jnp.sum(hits * source_place[:, :, None], 1)

    def slots_of(by_device):
        source_dev = device_of(
            lax.dynamic_index_in_dim(by_device, my_device, 0, keepdims=False)
        )
        onehot = (source_dev[:, None] == jnp.arange(dev_count, dtype=jnp.int32)[None, :]).astype(
            jnp.int32
        )
        slot_index = jnp.sum((ranks(onehot, 0) - onehot) * onehot, 1)
        return twin_of(source_dev), slot_index

    tables = [
        row_maps[channel]
        .reshape(pb_count, q_local, ka_count, row_count)
        .transpose(0, 2, 1, 3)
        .reshape(dev_count, local_count)
        for channel in range(2)
    ]
    chosen = jnp.stack([chosen_of(table) for table in tables]).reshape(2, local_count, 1)
    chosen = (chosen == jnp.arange(local_count, dtype=jnp.int32)).astype(jnp.bfloat16)
    send = select_rows(chosen, returned)
    received = lax.all_to_all(
        send.reshape(dev_count, per_peer, 4 * col_count), ("pb", "ka"), 0, 0, tiled=True
    ).reshape(local_count, 4 * col_count)

    ladder_out = total(place, vertex_ladder, [move(returned[d], twin_of) for d in range(q_local)])

    row_pick = []
    for channel in range(2):
        source_dev, slot_index = slots_of(tables[channel])
        slot = source_dev * per_peer + slot_index
        row_pick.append(slot[:, None] == jnp.arange(local_count, dtype=jnp.int32))
    crossed_a, crossed_b = place_rows(
        col_maps,
        jnp.stack(row_pick).astype(jnp.bfloat16),
        received,
        vertex_cross_a.reshape(2, local_count, col_count),
        vertex_cross_b.reshape(2, local_count, col_count),
    )
    return (
        ladder_out,
        crossed_a.reshape(vertex_cross_a.shape),
        crossed_b.reshape(vertex_cross_b.shape),
    )


def parts_of(q_local):
    return [(q_local - 1,), *((d,) for d in range(1, q_local - 1)), (0,)]


def solution(mesh):
    spread = P(None, "pb", "ka", None)

    return jax.shard_map(
        per_device,
        mesh=mesh,
        in_specs=(spread, spread, spread, P(None, "pb", None), P(), P()),
        out_specs=(spread, spread, spread),
        check_vma=False,
    )
```
